32 devices in a mesh: src: 8 (over z, y), tgt: 4 (over x, core).
Axes of the slice: x: 2, y: 2, z: 4, core: 2. Of those that a mesh axis runs over, the one named last changes fastest.
Arguments:
- edge_state: bfloat16 [65536, 512], P(('src', 'tgt')), may hold values from -6 to 6
- atom_state: bfloat16 [8192, 512], P('src'), may hold values from -6 to 6
- edge_src: int32 [65536], P(('src', 'tgt')), may hold values from 0 to 1023, as said below
- edge_tgt: int32 [65536], P(('src', 'tgt')), may hold values from 0 to 1023, as said below
- reverse: int32 [65536], P(('src', 'tgt')), may hold values from 0 to 2047, as said below
- w_in: bfloat16 [3, 512, 512], replicated, may hold values from -0.25 to 0.25
- w_out: bfloat16 [3, 512, 512], replicated, may hold values from -0.25 to 0.25
- edge_gain: float32 [3, 512], replicated, may hold values from 0.25 to 1.75
- atom_gain: float32 [512], replicated, may hold values from 0.25 to 1.75
- atom_up: bfloat16 [512, 512], replicated, may hold values from -0.25 to 0.25
- atom_down: bfloat16 [512, 512], replicated, may hold values from -0.25 to 0.25
Outputs:
- edge_out: bfloat16 [65536, 512], P(('src', 'tgt'))
The draws below stay inside these ranges and needn't reach their ends.
Inputs may be any that keep to these rules, and one draw needn't show every extreme that they name: edge_src is a local atom index within the edge's source block of 1024 atoms. edge_tgt is a local atom index within the edge's target block; the reverse edge's edge_src equals it. reverse is an involution on edges as defined in the reference program: the partner's partner is the edge itself, its source and target atoms are the edge's target and source, no edge is its own partner.
All inputs are finite; a program needn't handle non-finite values.
Results may differ from the reference program's by a relative error of at most 0.0075.
Values may be sent and summed in bfloat16 or wider, within the bound.
A program may use at most 64 MiB of HBM per device.

```python
import jax
import jax.numpy as jnp
from jax import lax

W = 512
BLOCKS = 3
E_DEV = 2048
AB = 1024
C = 2
Q = 128
ATOMS = 8192
EDGES = 65536
N_SRC = 8
N_TGT = 4


def graph_tables(key):
    count = N_SRC
    rows_sub = N_SRC * Q
    key_order = jax.random.fold_in(key, 11)
    key_ids = jax.random.fold_in(key, 12)
    scores = jax.random.randint(key_order, (count, count, rows_sub), 0, 65536) * rows_sub + jnp.arange(rows_sub, dtype=jnp.int32)
    order = jnp.argsort(scores, axis=-1).astype(jnp.int32)
    inverse = jnp.argsort(order, axis=-1).astype(jnp.int32)
    diagonal_pairs = jnp.take_along_axis(order, inverse ^ 1, axis=-1)
    first = jnp.arange(count, dtype=jnp.int32)[:, None, None]
    second = jnp.arange(count, dtype=jnp.int32)[None, :, None]
    pairing = jnp.where(first < second, order, jnp.where(first > second, jnp.transpose(inverse, (1, 0, 2)), diagonal_pairs))
    source_ids = jax.random.randint(key_ids, (count, count, rows_sub), 0, AB)
    target_ids = jnp.take_along_axis(jnp.transpose(source_ids, (1, 0, 2)), pairing, axis=-1)
    return (pairing, source_ids, target_ids)


def to_devices(table):
    shaped = table.reshape(N_SRC, N_TGT, C, N_SRC, Q)
    return jnp.transpose(shaped, (0, 1, 3, 2, 4)).reshape(-1).astype(jnp.int32)


def draw_edge_src(key, part):
    pairing, source_ids, target_ids = graph_tables(key)
    return to_devices(source_ids)


def draw_edge_tgt(key, part):
    pairing, source_ids, target_ids = graph_tables(key)
    return to_devices(target_ids)


def draw_reverse(key, part):
    pairing, source_ids, target_ids = graph_tables(key)
    subtile = (jnp.arange(N_SRC, dtype=jnp.int32) % C)[None, :, None]
    local = (pairing // Q * C + subtile) * Q + pairing % Q
    return to_devices(local)


def levels(rng, dims, pieces, low, high):
    loudness = 1.0
    for dim, blocks in pieces:
        steps = jax.random.uniform(jax.random.fold_in(jax.random.fold_in(rng, 6), dim), (blocks,), jnp.float32, low / len(pieces), high / len(pieces))
        loudness = loudness * jnp.repeat(jnp.exp(steps), dims[dim] // blocks).reshape((-1,) + (1,) * (len(dims) - 1 - dim))
    return loudness


def centred(own_key, extent, spread, limit, shards=(), kind=jnp.bfloat16):
    result = spread * jax.random.normal(own_key, extent, jnp.float32)
    if shards:
        result = result * levels(own_key, extent, shards, -0.22, 0.18)
    return jnp.clip(result, -limit, limit).astype(kind)


def setup_inputs(seed: int = 0) -> dict:
    key_of = jax.random.split(jax.random.key(seed), 12)
    return {
        "edge_state": centred(key_of[0], (EDGES, W), 1.0, 6.0, ((0, 32),)),
        "atom_state": centred(key_of[1], (ATOMS, W), 1.0, 6.0, ((0, 8),)),
        "edge_src": draw_edge_src(jax.random.fold_in(key_of[11], 71), 0),
        "edge_tgt": draw_edge_tgt(jax.random.fold_in(key_of[11], 71), 0),
        "reverse": draw_reverse(jax.random.fold_in(key_of[11], 71), 0),
        "w_in": centred(key_of[5], (BLOCKS, W, W), W ** -0.5, 0.25),
        "w_out": centred(key_of[6], (BLOCKS, W, W), W ** -0.5, 0.25),
        "edge_gain": jnp.clip(1.0 + 0.15 * jax.random.normal(key_of[7], (BLOCKS, W), jnp.float32), 0.25, 1.75),
        "atom_gain": jnp.clip(1.0 + 0.15 * jax.random.normal(key_of[8], (W,), jnp.float32), 0.25, 1.75),
        "atom_up": centred(key_of[9], (W, W), W ** -0.5, 0.25),
        "atom_down": centred(key_of[10], (W, W), W ** -0.5, 0.25),
    }


def rms_scaled(values, scales):
    return values * lax.rsqrt(lax.optimization_barrier(jnp.mean(values * values, axis=-1, keepdims=True)) + 1e-06) * scales

def reference(edge_state, atom_state, edge_src, edge_tgt, reverse, w_in, w_out, edge_gain, atom_gain, atom_up, atom_down):
    positions = jnp.arange(EDGES, dtype=jnp.int32)
    device_idx = positions // E_DEV
    local_pos = positions % E_DEV
    grid_row = device_idx // N_TGT
    grid_col = device_idx % N_TGT
    subtile = local_pos // Q % C
    source_atom = grid_row * AB + edge_src
    target_block = grid_col * C + subtile
    target_atom = (target_block * AB + edge_tgt).astype(jnp.int32)
    slice_idx = reverse // (C * Q)
    inner_row = reverse % Q
    partner = ((target_block * N_TGT + grid_row // C) * E_DEV + (slice_idx * C + grid_row % C) * Q + inner_row).astype(jnp.int32)
    initial = (edge_state.astype(jnp.float32) + atom_state[source_atom].astype(jnp.float32)).astype(jnp.bfloat16)
    mirrored = initial[partner]
    devices = N_SRC * N_TGT

    def edge_block(pair):
        start_rows, partner_rows = pair
        stream = start_rows.astype(jnp.float32)
        for layer in range(BLOCKS):
            normed = rms_scaled(stream, edge_gain[layer]).astype(jnp.bfloat16)
            hidden = jax.nn.silu(jnp.dot(normed, w_in[layer], preferred_element_type=jnp.float32)).astype(jnp.bfloat16)
            stream = stream + jnp.dot(hidden, w_out[layer], preferred_element_type=jnp.float32)
        return stream + partner_rows.astype(jnp.float32)
    merged = lax.map(edge_block, (initial.reshape(devices, E_DEV, W), mirrored.reshape(devices, E_DEV, W))).reshape(EDGES, W)
    message = merged.astype(jnp.bfloat16)
    atom_sum = jax.ops.segment_sum(message.astype(jnp.float32), target_atom, num_segments=ATOMS)
    atom_normed = rms_scaled(atom_sum, atom_gain).astype(jnp.bfloat16)
    atom_hidden = jax.nn.silu(jnp.dot(atom_normed, atom_up, preferred_element_type=jnp.float32)).astype(jnp.bfloat16)
    atom_new = jnp.dot(atom_hidden, atom_down, preferred_element_type=jnp.float32).astype(jnp.bfloat16)
    return (merged + atom_new[target_atom].astype(jnp.float32)).astype(jnp.bfloat16)
```

```python
import functools

import jax
import jax.numpy as jnp
from jax import lax
from jax.experimental import pallas as pl
from jax.experimental.pallas import tpu as pltpu
from jax.sharding import PartitionSpec as P

F32 = jnp.float32
BF16 = jnp.bfloat16
MESH = pl.DeviceIdType.MESH


def rms_scaled(values, scales):
    return values * lax.rsqrt(jnp.mean(values * values, axis=-1, keepdims=True) + 1e-06) * scales


def whole_kernel(
    plan,
    edge_ref,
    atom_ref,
    src_ref,
    tgt_ref,
    rev_ref,
    w_in_ref,
    w_out_ref,
    gain_ref,
    atom_gain_ref,
    up_ref,
    down_ref,
    out_ref,
    start,
    stream,
    recv,
    relay,
    message,
    part,
    box,
    pack,
    fresh,
    send_sems,
    recv_sems,
    relay_sems,
    forward_sems,
    sum_sems,
    share_sems,
):
    n_src, n_tgt, groups = plan["n_src"], plan["n_tgt"], plan["groups"]
    slices, _, rows_sub, width = edge_ref.shape
    rows = slices * rows_sub
    atoms = atom_ref.shape[0]
    layers = w_in_ref.shape[0]
    half = n_tgt // 2
    chunks = slices
    relayed = chunks // 2
    i = lax.axis_index("src")
    j = lax.axis_index("tgt")
    home = i // groups
    phase = lax.rem(i, groups)
    on_path = j // 2 == home // 2
    off_path = jnp.logical_not(on_path)
    away = [i != j * groups + g for g in range(groups)]

    def remote(source, target, send_sem, recv_sem, row, col):
        return pltpu.make_async_remote_copy(
            src_ref=source,
            dst_ref=target,
            send_sem=send_sem,
            recv_sem=recv_sem,
            device_id={"src": row, "tgt": col},
            device_id_type=MESH,
        )

    radix = {"y": 2, "p": 2, "c": n_src // 4}
    scale = {"y": 1, "p": 2, "c": 4}
    digit = {"y": lax.rem(i, 2), "p": lax.rem(i // 2, 2), "c": i // 4}

    def peer(dim, offset):
        turned = lax.rem(digit[dim] + offset, radix[dim])
        return i + (turned - digit[dim]) * scale[dim]

    barrier = pltpu.get_barrier_semaphore()

    def greet(row, col):
        pl.semaphore_signal(barrier, inc=1, device_id={"src": row, "tgt": col}, device_id_type=MESH)

    count = jnp.int32(0)
    for dim in "ypc":
        for offset in range(1, radix[dim]):
            greet(peer(dim, offset), j)
            count += 1
    for g in range(groups):

        @pl.when(away[g])
        def _():
            greet(j * groups + g, home)

        count += away[g].astype(jnp.int32)

        @pl.when(off_path)
        def _():
            greet(j * groups + g, j // 2 * 2 + lax.rem(home, 2))

    for slot in range(half - 1):
        source_col = lax.rem(j // 2 + slot + 1, half) * 2 + lax.rem(j, 2)

        @pl.when(on_path)
        def _():
            greet(i, source_col)

    count += jnp.where(on_path, (half - 1) * groups, 1)
    pl.semaphore_wait(barrier, count)

    src_cols = src_ref[...].T
    reverse = rev_ref[...]
    rev_cols = (lax.div(reverse, groups * rows_sub) * rows_sub + lax.rem(reverse, rows_sub)).T
    tgt_cols = tgt_ref[...].T

    def tile_column(cols, g, first, number):
        return jnp.concatenate(
            [cols[:, n * groups + g : n * groups + g + 1] for n in range(first, first + number)], axis=0
        )

    def chosen(column, slots):
        return jnp.where(column == slots, 1.0, 0.0).astype(BF16)

    atom_slots = lax.broadcasted_iota(jnp.int32, (1, atoms), 1)
    row_slots = lax.broadcasted_iota(jnp.int32, (1, rows), 1)

    def chunk_rows(k, number=1):
        return pl.ds(k * rows_sub, number * rows_sub)

    def permute_copy(g, k, direct):
        source = start.at[g, chunk_rows(k)]
        if direct:
            return remote(
                source, recv.at[phase, chunk_rows(k)], send_sems.at[g, k], recv_sems.at[phase, k], j * groups + g, home
            )
        slot = lax.rem(j // 2 - home // 2 + half, half) - 1
        slot = jnp.maximum(slot, 0)
        return remote(
            source,
            relay.at[slot, g, chunk_rows(k)],
            send_sems.at[g, k],
            relay_sems.at[slot, g, k],
            i,
            home // 2 * 2 + lax.rem(j, 2),
        )

    def permute_send(g, k, allowed):
        if k < relayed:

            @pl.when(jnp.logical_and(allowed, off_path))
            def _():
                permute_copy(g, k, False).start()

            @pl.when(jnp.logical_and(jnp.logical_and(allowed, on_path), away[g]))
            def _():
                permute_copy(g, k, True).start()
        else:

            @pl.when(jnp.logical_and(allowed, away[g]))
            def _():
                permute_copy(g, k, True).start()

    def forward_copy(slot, g, k):
        column = lax.rem(j // 2 + slot + 1, half) * 2 + lax.rem(j, 2)
        return remote(
            relay.at[slot, g, chunk_rows(k)],
            recv.at[phase, chunk_rows(k)],
            forward_sems.at[slot, g, k],
            recv_sems.at[phase, k],
            column * groups + g,
            home,
        )

    def arrival(slot, g, k):
        return remote(
            relay.at[slot, g, chunk_rows(k)],
            relay.at[slot, g, chunk_rows(k)],
            forward_sems.at[slot, g, k],
            relay_sems.at[slot, g, k],
            i,
            lax.rem(j + 2, n_tgt),
        )

    def forward(g, k, allowed):
        for slot in range(half - 1):

            @pl.when(jnp.logical_and(allowed, on_path))
            def _():
                arrival(slot, g, k).wait_recv()
                forward_copy(slot, g, k).start()

    batch = plan["batch"]
    split = relayed // batch
    spots = []
    for n in range(split):
        spots += [n * batch, relayed + n * batch]
    for first in spots:
        for g in range(groups):
            column = tile_column(src_cols, g, first, batch)
            sources = jnp.dot(chosen(column, atom_slots), atom_ref[...], preferred_element_type=F32)
            edges = edge_ref[first : first + batch, g].reshape(batch * rows_sub, width).astype(F32)
            value = (edges + sources).astype(BF16)
            start[g, chunk_rows(first, batch)] = value

            @pl.when(jnp.logical_not(away[g]))
            def _():
                recv[g, chunk_rows(first, batch)] = value

            for k in range(first, first + batch):
                permute_send(g, k, phase == 0)

    wide = plan["wide"]
    queue = [(g, k) for k in range(relayed) for g in range(groups)]
    early, late = list(queue), list(queue)

    def stream_tile(g, first):
        values = start[g, pl.ds(first, wide)].astype(F32)
        for layer in range(layers):
            normed = rms_scaled(values, gain_ref[layer : layer + 1]).astype(BF16)
            hidden = jax.nn.silu(jnp.dot(normed, w_in_ref[layer], preferred_element_type=F32)).astype(BF16)
            values = values + jnp.dot(hidden, w_out_ref[layer], preferred_element_type=F32)
        stream[g, pl.ds(first, wide)] = values

    tiles = [(g, first) for g in range(groups) for first in range(0, rows, wide)]
    for n, (g, first) in enumerate(tiles):
        stream_tile(g, first)
        for _ in range(len(queue) // len(tiles) if n < len(tiles) - 1 else len(early)):
            forward(*early.pop(0), phase == 0)
    for first in spots:
        for g in range(groups):
            for k in range(first, first + batch):
                for p in range(1, groups):
                    permute_send(g, k, phase == p)

    def drain_late(number):
        for _ in range(min(number, len(late))):
            g, k = late.pop(0)
            for p in range(1, groups):
                forward(g, k, phase == p)

    def merge(g):
        for k in range(chunks):

            @pl.when(away[g])
            def _():
                remote(
                    start.at[g, chunk_rows(k)],
                    recv.at[g, chunk_rows(k)],
                    send_sems.at[g, k],
                    recv_sems.at[g, k],
                    peer("y", 1),
                    j,
                ).wait_recv()

        for first in range(0, chunks, batch):
            column = tile_column(rev_cols, g, first, batch)
            partner = jnp.dot(chosen(column, row_slots), recv[g], preferred_element_type=F32)
            merged = stream[g, chunk_rows(first, batch)] + partner
            stream[g, chunk_rows(first, batch)] = merged
            message[g, chunk_rows(first, batch)] = merged.astype(BF16)

    def scatter(g):
        line = jnp.concatenate([tgt_ref[n * groups + g : n * groups + g + 1, :] for n in range(slices)], axis=1)
        tall = plan["tall"]
        for first in range(0, atoms, tall):
            slots = lax.broadcasted_iota(jnp.int32, (tall, rows), 0) + first
            picks = jnp.where(slots == line, 1.0, 0.0).astype(BF16)
            part[g, pl.ds(first, tall)] = jnp.dot(picks, message[g], preferred_element_type=F32).astype(BF16)

    class Piece:
        pass

    pieces = []
    sums, shares, boxes, packs = 0, 0, 0, 0
    for g, base, size, order in plan["parts"]:
        piece = Piece()
        piece.g, piece.base, piece.size, piece.order = g, base, size, order
        piece.n = [radix[dim] for dim in order]
        piece.d = [digit[dim] for dim in order]
        piece.unit = [size]
        for n in piece.n:
            piece.unit.append(piece.unit[-1] // n)
        piece.origin = [jnp.int32(base)]
        for level in range(3):
            piece.origin.append(piece.origin[-1] + piece.d[level] * piece.unit[level + 1])
        piece.box, piece.pack, piece.sum = [], [], []
        for level in range(3):
            piece.box.append(boxes)
            piece.pack.append(packs)
            piece.sum.append(sums)
            boxes += (piece.n[level] - 1) * piece.unit[level + 1]
            packs += (piece.n[level] - 1) * piece.unit[level + 1] if level else 0
            sums += (piece.n[level] - 1) * (piece.n[level + 1] if level < 2 else 1)
        piece.share = shares
        shares += 2 * n_src
        pieces.append(piece)

    def aligned(value):
        return pl.multiple_of(value, 16)

    def value_at(piece, level, origin, size):
        total = part[piece.g, pl.ds(aligned(origin), size)].astype(F32)
        for lower in range(level):
            for offset in range(1, piece.n[lower]):
                place = piece.box[lower] + (offset - 1) * piece.unit[lower + 1] + origin - piece.origin[lower + 1]
                total = total + box[pl.ds(aligned(place), size)].astype(F32)
        return total

    def sum_steps(piece, level):
        unit = piece.unit[level + 1]
        fan = piece.n[level + 1] if level < 2 else 1
        inner = unit // fan
        for turn in range(fan):
            for offset in range(1, piece.n[level]):
                theirs = lax.rem(piece.d[level] + offset, piece.n[level])
                if level < 2:
                    spot = lax.rem(piece.d[level + 1] + turn + 1, fan) * inner
                else:
                    spot = jnp.int32(0)
                yield turn, offset, piece.origin[level] + theirs * unit + spot, spot, inner

    def sum_copy(piece, level, turn, offset, origin, spot, inner):
        fan = piece.n[level + 1] if level < 2 else 1
        if level == 0:
            source = part.at[piece.g, pl.ds(aligned(origin), inner)]
        else:
            place = piece.pack[level] + (offset - 1) * piece.unit[level + 1] + spot
            source = pack.at[pl.ds(aligned(place), inner)]
        target = box.at[pl.ds(aligned(piece.box[level] + (offset - 1) * piece.unit[level + 1] + spot), inner)]
        index = piece.sum[level] + (offset - 1) * fan + turn
        return remote(source, target, sum_sems.at[0, index], sum_sems.at[1, index], peer(piece.order[level], offset), j)

    def sum_wait(piece, level, turn):
        for step in sum_steps(piece, level):
            if step[0] == turn:
                sum_copy(piece, level, *step).wait_recv()

    def sum_send(piece, level):
        ready = set()
        fan = piece.n[level]
        for step in sum_steps(piece, level):
            turn, offset, origin, spot, inner = step
            if level:
                need = (offset - 1) % fan
                if need not in ready:
                    ready.add(need)
                    sum_wait(piece, level - 1, need)
                    if level > 1:
                        pass
                place = piece.pack[level] + (offset - 1) * piece.unit[level + 1] + spot
                pack[pl.ds(aligned(place), inner)] = value_at(piece, level, origin, inner).astype(BF16)
            sum_copy(piece, level, *step).start()
        if level:
            for turn in range(fan):
                if turn not in ready:
                    ready.add(turn)
                    piece_last = turn
                    sum_wait(piece, level - 1, piece_last)

    def sum_last(piece):
        sum_wait(piece, 2, 0)
        return value_at(piece, 3, piece.origin[3], piece.unit[3])

    def share_index(piece, offsets, dim_level):
        n = piece.n
        return ((offsets[0] * n[1]) + offsets[1]) * n[2] + offsets[2]

    def share_copy(piece, offsets, level, offset):
        origin = jnp.int32(piece.base)
        for low in range(3):
            owner = lax.rem(piece.d[low] - offsets[low] + piece.n[low], piece.n[low])
            origin = origin + owner * piece.unit[low + 1]
        there = list(offsets)
        there[level] = offset
        index = piece.share + share_index(piece, there, level)
        window = fresh.at[piece.g, pl.ds(aligned(origin), piece.unit[3])]
        return remote(window, window, share_sems.at[0, index], share_sems.at[1, index], peer(piece.order[level], offset), j)

    def held(piece, level):
        n = piece.n
        result = []
        for own in range(1, n[level]):
            options = [(0,), (0,), (0,)]
            options[level] = (own,)
            for high in range(level + 1, 3):
                options[high] = tuple(range(n[high]))
            result += [(a, b, c) for a in options[0] for b in options[1] for c in options[2]]
        return sorted(result, key=lambda offsets: tuple(reversed(offsets)))

    def share_all(piece, offsets, below):
        for level in reversed(range(below)):
            for offset in range(1, piece.n[level]):
                share_copy(piece, offsets, level, offset).start()

    def share_wait(piece, offsets):
        origin = jnp.int32(piece.base)
        for low in range(3):
            owner = lax.rem(piece.d[low] - offsets[low] + piece.n[low], piece.n[low])
            origin = origin + owner * piece.unit[low + 1]
        index = piece.share + share_index(piece, offsets, None)
        window = fresh.at[piece.g, pl.ds(aligned(origin), piece.unit[3])]
        remote(window, window, share_sems.at[0, index], share_sems.at[1, index], peer("y", 1), j).wait_recv()

    def share_forward(piece, level):
        for offsets in held(piece, level):
            share_wait(piece, offsets)
            share_all(piece, offsets, level)

    def of_block(g):
        return [piece for piece in pieces if piece.g == g]

    def update(g):
        mine = of_block(g)
        total = jnp.concatenate([sum_last(piece) for piece in mine], axis=0)
        normed = rms_scaled(total, atom_gain_ref[...]).astype(BF16)
        hidden = jax.nn.silu(jnp.dot(normed, up_ref[...], preferred_element_type=F32)).astype(BF16)
        new = jnp.dot(hidden, down_ref[...], preferred_element_type=F32).astype(BF16)
        first = 0
        for piece in mine:
            fresh[g, pl.ds(aligned(piece.origin[3]), piece.unit[3])] = new[first : first + piece.unit[3]]
            first += piece.unit[3]
        for piece in mine:
            share_all(piece, (0, 0, 0), 3)

    def finish(g):
        for first in range(0, chunks, batch):
            column = tile_column(tgt_cols, g, first, batch)
            returned = jnp.dot(chosen(column, atom_slots), fresh[g], preferred_element_type=F32)
            value = (stream[g, chunk_rows(first, batch)] + returned).astype(BF16)
            out_ref[first : first + batch, g] = value.reshape(batch, rows_sub, width)

    def level_send(g, level):
        for piece in of_block(g):
            sum_send(piece, level)

    def level_forward(g, level):
        for piece in of_block(g):
            share_forward(piece, level)

    last = groups - 1
    for g in range(groups):
        merge(g)
        scatter(g)
        level_send(g, 0)
        if g < last:
            drain_late(2)
            level_send(g, 1)
            drain_late(2)
            level_send(g, 2)
            drain_late(len(late))
            update(g)
    level_send(last, 1)
    for g in range(last):
        level_forward(g, 2)
    level_send(last, 2)
    for g in range(last):
        level_forward(g, 1)
    update(last)
    for g in range(last):
        level_forward(g, 0)
        finish(g)
    level_forward(last, 2)
    level_forward(last, 1)
    level_forward(last, 0)
    finish(last)

    for g in range(groups):
        for k in range(chunks):
            if k < relayed:

                @pl.when(off_path)
                def _():
                    permute_copy(g, k, False).wait_send()

                for slot in range(half - 1):

                    @pl.when(on_path)
                    def _():
                        forward_copy(slot, g, k).wait_send()

                @pl.when(jnp.logical_and(on_path, away[g]))
                def _():
                    permute_copy(g, k, True).wait_send()
            else:

                @pl.when(away[g])
                def _():
                    permute_copy(g, k, True).wait_send()

    for piece in pieces:
        for level in range(3):
            for step in sum_steps(piece, level):
                sum_copy(piece, level, *step).wait_send()
        for offsets in [(0, 0, 0)] + held(piece, 2) + held(piece, 1):
            below = 3 if offsets == (0, 0, 0) else 2 if offsets in held(piece, 2) else 1
            for level in range(below):
                for offset in range(1, piece.n[level]):
                    share_copy(piece, offsets, level, offset).wait_send()


def shards(
    edge_state,
    atom_state,
    edge_src,
    edge_tgt,
    reverse,
    w_in,
    w_out,
    edge_gain,
    atom_gain,
    atom_up,
    atom_down,
):
    n_src = lax.axis_size("src")
    n_tgt = lax.axis_size("tgt")
    groups = n_src // n_tgt
    edge_rows, width = edge_state.shape
    atoms = atom_state.shape[0]
    rows_sub = edge_rows // (groups * n_src)
    rows = n_src * rows_sub
    parts = [(g, 0, atoms, "ypc") for g in range(groups)]
    plan = {
        "n_src": n_src,
        "n_tgt": n_tgt,
        "groups": groups,
        "parts": parts,
        "batch": 2,
        "wide": min(rows, 512),
        "tall": min(atoms, 256),
    }
    radix = {"y": 2, "p": 2, "c": n_src // 4}
    boxes, packs, sums = 0, 0, 0
    for g, base, size, order in parts:
        n = [radix[dim] for dim in order]
        unit = size
        for level in range(3):
            unit //= n[level]
            boxes += (n[level] - 1) * unit
            packs += (n[level] - 1) * unit if level else 0
            sums += (n[level] - 1) * (n[level + 1] if level < 2 else 1)
    half = n_tgt // 2
    dma = pltpu.SemaphoreType.DMA
    whole = pl.BlockSpec(memory_space=pltpu.VMEM)

    def lines(index):
        return index.reshape(n_src * groups, rows_sub)

    framed = edge_state.reshape(n_src, groups, rows_sub, width)
    out = pl.pallas_call(
        functools.partial(whole_kernel, plan),
        name="block",
        in_specs=[whole] * 11,
        out_specs=whole,
        out_shape=jax.ShapeDtypeStruct(framed.shape, BF16),
        scratch_shapes=[
            pltpu.VMEM((groups, rows, width), BF16),
            pltpu.VMEM((groups, rows, width), F32),
            pltpu.VMEM((groups, rows, width), BF16),
            pltpu.VMEM((half - 1, groups, rows // 2, width), BF16),
            pltpu.VMEM((groups, rows, width), BF16),
            pltpu.VMEM((groups, atoms, width), BF16),
            pltpu.VMEM((boxes, width), BF16),
            pltpu.VMEM((packs, width), BF16),
            pltpu.VMEM((groups, atoms, width), BF16),
            dma((groups, n_src)),
            dma((groups, n_src)),
            dma((half - 1, groups, n_src // 2)),
            dma((half - 1, groups, n_src // 2)),
            dma((2, sums)),
            dma((2, len(parts) * 2 * n_src)),
        ],
        compiler_params=pltpu.CompilerParams(
            collective_id=0, has_side_effects=True, vmem_limit_bytes=56 * 2**20
        ),
    )(
        framed,
        atom_state,
        lines(edge_src),
        lines(edge_tgt),
        lines(reverse),
        w_in,
        w_out,
        edge_gain,
        atom_gain.reshape(1, width),
        atom_up,
        atom_down,
    )
    return out.reshape(edge_rows, width)


def solution(mesh):
    in_specs = (
        P(("src", "tgt"), None),
        P("src", None),
        P(("src", "tgt")),
        P(("src", "tgt")),
        P(("src", "tgt")),
        P(),
        P(),
        P(),
        P(),
        P(),
        P(),
    )
    out_specs = P(("src", "tgt"), None)
    return jax.shard_map(shards, mesh=mesh, in_specs=in_specs, out_specs=out_specs, check_vma=False)
```

```python
import functools

import jax
import jax.numpy as jnp
from jax import lax
from jax.experimental import pallas as pl
from jax.experimental.pallas import tpu as pltpu
from jax.sharding import PartitionSpec as P

F32 = jnp.float32
BF16 = jnp.bfloat16
MESH = pl.DeviceIdType.MESH


def rms_scaled(values, scales):
    return values * lax.rsqrt(jnp.mean(values * values, axis=-1, keepdims=True) + 1e-06) * scales


def whole_kernel(
    plan,
    edge_ref,
    atom_ref,
    src_ref,
    tgt_ref,
    rev_ref,
    w_in_ref,
    w_out_ref,
    gain_ref,
    atom_gain_ref,
    up_ref,
    down_ref,
    out_ref,
    start,
    stream,
    recv,
    relay,
    message,
    part,
    box,
    pack,
    fresh,
    row_part,
    row_pack,
    row_box,
    send_sems,
    recv_sems,
    relay_sems,
    forward_sems,
    sum_sems,
    share_sems,
    row_sems,
):
    n_src, n_tgt, groups = plan["n_src"], plan["n_tgt"], plan["groups"]
    slices, _, rows_sub, width = edge_ref.shape
    rows = slices * rows_sub
    atoms = atom_ref.shape[0]
    layers = w_in_ref.shape[0]
    half = n_tgt // 2
    chunks = slices
    relayed = chunks // 2
    i = lax.axis_index("src")
    j = lax.axis_index("tgt")
    home = i // groups
    phase = lax.rem(i, groups)
    on_path = j // 2 == home // 2
    off_path = jnp.logical_not(on_path)
    away = [i != j * groups + g for g in range(groups)]

    def remote(source, target, send_sem, recv_sem, row, col):
        return pltpu.make_async_remote_copy(
            src_ref=source,
            dst_ref=target,
            send_sem=send_sem,
            recv_sem=recv_sem,
            device_id={"src": row, "tgt": col},
            device_id_type=MESH,
        )

    radix = {"y": 2, "p": 2, "c": n_src // 4}
    scale = {"y": 1, "p": 2, "c": 4}
    digit = {"y": lax.rem(i, 2), "p": lax.rem(i // 2, 2), "c": i // 4}

    def peer(dim, offset):
        turned = lax.rem(digit[dim] + offset, radix[dim])
        return i + (turned - digit[dim]) * scale[dim]

    barrier = pltpu.get_barrier_semaphore()

    def greet(row, col):
        pl.semaphore_signal(barrier, inc=1, device_id={"src": row, "tgt": col}, device_id_type=MESH)

    greet(i, j + 1 - 2 * lax.rem(j, 2))
    count = jnp.int32(1)
    for dim in "ypc":
        for offset in range(1, radix[dim]):
            greet(peer(dim, offset), j)
            count += 1
    for g in range(groups):

        @pl.when(away[g])
        def _():
            greet(j * groups + g, home)

        count += away[g].astype(jnp.int32)

        @pl.when(off_path)
        def _():
            greet(j * groups + g, j // 2 * 2 + lax.rem(home, 2))

    for slot in range(half - 1):
        source_col = lax.rem(j // 2 + slot + 1, half) * 2 + lax.rem(j, 2)

        @pl.when(on_path)
        def _():
            greet(i, source_col)

    count += jnp.where(on_path, (half - 1) * groups, 1)
    src_cols = src_ref[...].T
    reverse = rev_ref[...]
    rev_cols = (lax.div(reverse, groups * rows_sub) * rows_sub + lax.rem(reverse, rows_sub)).T
    tgt_cols = tgt_ref[...].T

    def tile_column(cols, g, first, number):
        return jnp.concatenate(
            [cols[:, n * groups + g : n * groups + g + 1] for n in range(first, first + number)], axis=0
        )

    def chosen(column, slots):
        return jnp.where(column == slots, 1.0, 0.0).astype(BF16)

    atom_slots = lax.broadcasted_iota(jnp.int32, (1, atoms), 1)
    row_slots = lax.broadcasted_iota(jnp.int32, (1, rows), 1)

    def chunk_rows(k, number=1):
        return pl.ds(k * rows_sub, number * rows_sub)

    def permute_copy(g, k, direct):
        source = start.at[g, chunk_rows(k)]
        if direct:
            return remote(
                source, recv.at[phase, chunk_rows(k)], send_sems.at[g, k], recv_sems.at[phase, k], j * groups + g, home
            )
        slot = lax.rem(j // 2 - home // 2 + half, half) - 1
        slot = jnp.maximum(slot, 0)
        return remote(
            source,
            relay.at[slot, g, chunk_rows(k)],
            send_sems.at[g, k],
            relay_sems.at[slot, g, k],
            i,
            home // 2 * 2 + lax.rem(j, 2),
        )

    def permute_send(g, k):
        if k < relayed:

            @pl.when(off_path)
            def _():
                permute_copy(g, k, False).start()

            @pl.when(jnp.logical_and(on_path, away[g]))
            def _():
                permute_copy(g, k, True).start()
        else:

            @pl.when(away[g])
            def _():
                permute_copy(g, k, True).start()

    def forward_copy(slot, g, k):
        column = lax.rem(j // 2 + slot + 1, half) * 2 + lax.rem(j, 2)
        return remote(
            relay.at[slot, g, chunk_rows(k)],
            recv.at[phase, chunk_rows(k)],
            forward_sems.at[slot, g, k],
            recv_sems.at[phase, k],
            column * groups + g,
            home,
        )

    def arrival(slot, g, k):
        return remote(
            relay.at[slot, g, chunk_rows(k)],
            relay.at[slot, g, chunk_rows(k)],
            forward_sems.at[slot, g, k],
            relay_sems.at[slot, g, k],
            i,
            lax.rem(j + 2, n_tgt),
        )

    def forward(g, k):
        for slot in range(half - 1):

            @pl.when(on_path)
            def _():
                arrival(slot, g, k).wait_recv()
                forward_copy(slot, g, k).start()

    batch = plan["batch"]
    for first in range(0, chunks, batch):
        for g in range(groups):
            column = tile_column(src_cols, g, first, batch)
            sources = jnp.dot(chosen(column, atom_slots), atom_ref[...], preferred_element_type=F32)
            edges = edge_ref[first : first + batch, g].reshape(batch * rows_sub, width).astype(F32)
            value = (edges + sources).astype(BF16)
            start[g, chunk_rows(first, batch)] = value

            @pl.when(jnp.logical_not(away[g]))
            def _():
                recv[g, chunk_rows(first, batch)] = value

    pl.semaphore_wait(barrier, count)

    steps = [(g, k) for k in range(relayed) for g in range(groups)]
    behind = []

    def pump(number):
        for _ in range(number):
            if behind:
                forward(*behind.pop(0))
            if steps:
                g, k = steps.pop(0)
                permute_send(g, k)
                permute_send(g, relayed + k)
                behind.append((g, k))

    tall = plan["tall"]
    core = lax.rem(j, 2)
    half_atoms = atoms // 2
    is_root = home == j
    is_helper = jnp.logical_and(on_path, jnp.logical_not(is_root))

    def aligned(value):
        return pl.multiple_of(value, 16)

    def index_line(ref, g):
        return jnp.concatenate([ref[pl.ds(n * groups + g, 1), :] for n in range(slices)], axis=1)

    def picks(line, first):
        slots = lax.broadcasted_iota(jnp.int32, (tall, line.shape[1]), 0) + first
        return jnp.where(slots == line, 1.0, 0.0).astype(BF16)

    def half_rows(which):
        return pl.ds(aligned(which * half_atoms), half_atoms)

    def core_copy():
        return remote(
            row_part.at[half_rows(1 - core)], row_box.at[0], row_sems.at[0, 0], row_sems.at[1, 0], i, j + 1 - 2 * core
        )

    def across_copy():
        slot = jnp.maximum(lax.rem(j // 2 - home // 2 + half, half) - 1, 0)
        return remote(
            row_pack, row_box.at[2 + slot], row_sems.at[0, 1], row_sems.at[1, 2 + slot], i, home // 2 * 2 + core
        )

    def helper_copy():
        return remote(row_pack, row_box.at[1], row_sems.at[0, 1], row_sems.at[1, 1], i, home)

    def row_scatter():
        lines = [index_line(src_ref, g) for g in range(groups)]
        for first in range(0, atoms, tall):
            total = jnp.dot(picks(lines[0], first), start[0], preferred_element_type=F32)
            for g in range(1, groups):
                total = total + jnp.dot(picks(lines[g], first), start[g], preferred_element_type=F32)
            row_part[pl.ds(first, tall)] = total.astype(BF16)
        core_copy().start()

    def row_across():
        core_copy().wait()

        @pl.when(off_path)
        def _():
            row_pack[...] = (row_part[half_rows(core)].astype(F32) + row_box[0].astype(F32)).astype(BF16)
            across_copy().start()

    def row_total():
        total = row_part[half_rows(core)].astype(F32) + row_box[0].astype(F32)
        for slot in range(half - 1):
            total = total + row_box[2 + slot].astype(F32)
        return total

    def row_gather():
        for slot in range(half - 1):

            @pl.when(on_path)
            def _():
                remote(
                    row_pack, row_box.at[2 + slot], row_sems.at[0, 1], row_sems.at[1, 2 + slot], i, j + 1 - 2 * core
                ).wait_recv()

        @pl.when(is_helper)
        def _():
            row_pack[...] = row_total().astype(BF16)
            helper_copy().start()

    def row_add():
        @pl.when(is_root)
        def _():
            mine, other = half_rows(core), half_rows(1 - core)
            part[phase, mine] = (part[phase, mine].astype(F32) + row_total()).astype(BF16)
            remote(
                row_pack, row_box.at[1], row_sems.at[0, 1], row_sems.at[1, 1], i, j + 1 - 2 * core
            ).wait_recv()
            part[phase, other] = (part[phase, other].astype(F32) + row_box[1].astype(F32)).astype(BF16)

    wide = plan["wide"]

    def stream_tile(g, first):
        values = start[g, pl.ds(first, wide)].astype(F32)
        for layer in range(layers):
            normed = rms_scaled(values, gain_ref[layer : layer + 1]).astype(BF16)
            hidden = jax.nn.silu(jnp.dot(normed, w_in_ref[layer], preferred_element_type=F32)).astype(BF16)
            values = values + jnp.dot(hidden, w_out_ref[layer], preferred_element_type=F32)
        stream[g, pl.ds(first, wide)] = values
        message[g, pl.ds(first, wide)] = values.astype(BF16)

    def scatter(g):
        line = index_line(tgt_ref, g)
        for first in range(0, atoms, tall):
            part[g, pl.ds(first, tall)] = jnp.dot(
                picks(line, first), message[g], preferred_element_type=F32
            ).astype(BF16)

    class Piece:
        pass

    pieces = []
    sums, shares, boxes, packs = 0, 0, 0, 0
    for k, base, size, order in plan["parts"]:
        piece = Piece()
        piece.k, piece.base, piece.size, piece.order = k, base, size, order
        piece.g, piece.next = lax.rem(i + k, groups), lax.rem(i + k + 1, groups)
        piece.n = [radix[dim] for dim in order]
        piece.d = [digit[dim] for dim in order]
        piece.unit = [size]
        for n in piece.n:
            piece.unit.append(piece.unit[-1] // n)
        piece.origin = [jnp.int32(base)]
        for level in range(3):
            piece.origin.append(piece.origin[-1] + piece.d[level] * piece.unit[level + 1])
        piece.box, piece.pack, piece.sum = [], [], []
        for level in range(3):
            piece.box.append(boxes)
            piece.pack.append(packs)
            piece.sum.append(sums)
            boxes += (piece.n[level] - 1) * piece.unit[level + 1]
            packs += (piece.n[level] - 1) * piece.unit[level + 1] if level else 0
            sums += (piece.n[level] - 1) * (piece.n[level + 1] if level < 2 else 1)
        piece.share = shares
        shares += n_src
        pieces.append(piece)

    def value_at(piece, level, origin, size):
        total = part[piece.g, pl.ds(aligned(origin), size)].astype(F32)
        for lower in range(level):
            for offset in range(1, piece.n[lower]):
                place = piece.box[lower] + (offset - 1) * piece.unit[lower + 1] + origin - piece.origin[lower + 1]
                total = total + box[pl.ds(aligned(place), size)].astype(F32)
        return total

    def sum_steps(piece, level):
        unit = piece.unit[level + 1]
        fan = piece.n[level + 1] if level < 2 else 1
        inner = unit // fan
        for turn in range(fan):
            for offset in range(1, piece.n[level]):
                theirs = lax.rem(piece.d[level] + offset, piece.n[level])
                if level < 2:
                    spot = lax.rem(piece.d[level + 1] + turn + 1, fan) * inner
                else:
                    spot = jnp.int32(0)
                yield turn, offset, piece.origin[level] + theirs * unit + spot, spot, inner

    def sum_copy(piece, level, turn, offset, origin, spot, inner):
        fan = piece.n[level + 1] if level < 2 else 1
        if level == 0:
            source = part.at[piece.next, pl.ds(aligned(origin), inner)]
        else:
            place = piece.pack[level] + (offset - 1) * piece.unit[level + 1] + spot
            source = pack.at[pl.ds(aligned(place), inner)]
        target = box.at[pl.ds(aligned(piece.box[level] + (offset - 1) * piece.unit[level + 1] + spot), inner)]
        index = piece.sum[level] + (offset - 1) * fan + turn
        return remote(source, target, sum_sems.at[0, index], sum_sems.at[1, index], peer(piece.order[level], offset), j)

    def sum_wait(piece, level, turn):
        for step in sum_steps(piece, level):
            if step[0] == turn:
                sum_copy(piece, level, *step).wait_recv()

    def sum_send(piece, level):
        ready = set()
        fan = piece.n[level]
        for step in sum_steps(piece, level):
            turn, offset, origin, spot, inner = step
            if level:
                need = (offset - 1) % fan
                if need not in ready:
                    ready.add(need)
                    sum_wait(piece, level - 1, need)
                    if level > 1:
                        pass
                place = piece.pack[level] + (offset - 1) * piece.unit[level + 1] + spot
                pack[pl.ds(aligned(place), inner)] = value_at(piece, level, origin, inner).astype(BF16)
            sum_copy(piece, level, *step).start()
        if level:
            for turn in range(fan):
                if turn not in ready:
                    ready.add(turn)
                    piece_last = turn
                    sum_wait(piece, level - 1, piece_last)

    def sum_last(piece):
        sum_wait(piece, 2, 0)
        return value_at(piece, 3, piece.origin[3], piece.unit[3])

    def share_index(piece, offsets, dim_level):
        n = piece.n
        return ((offsets[0] * n[1]) + offsets[1]) * n[2] + offsets[2]

    def share_copy(piece, offsets, level, offset):
        origin = jnp.int32(piece.base)
        for low in range(3):
            owner = lax.rem(piece.d[low] - offsets[low] + piece.n[low], piece.n[low])
            origin = origin + owner * piece.unit[low + 1]
        there = list(offsets)
        there[level] = offset
        index = piece.share + share_index(piece, there, level)
        window = fresh.at[piece.g, pl.ds(aligned(origin), piece.unit[3])]
        return remote(window, window, share_sems.at[0, index], share_sems.at[1, index], peer(piece.order[level], offset), j)

    def held(piece, level):
        n = piece.n
        result = []
        for own in range(1, n[level]):
            options = [(0,), (0,), (0,)]
            options[level] = (own,)
            for high in range(level + 1, 3):
                options[high] = tuple(range(n[high]))
            result += [(a, b, c) for a in options[0] for b in options[1] for c in options[2]]
        return sorted(result, key=lambda offsets: tuple(reversed(offsets)))

    def share_all(piece, offsets, below):
        for level in reversed(range(below)):
            for offset in range(1, piece.n[level]):
                share_copy(piece, offsets, level, offset).start()

    def share_wait(piece, offsets):
        origin = jnp.int32(piece.base)
        for low in range(3):
            owner = lax.rem(piece.d[low] - offsets[low] + piece.n[low], piece.n[low])
            origin = origin + owner * piece.unit[low + 1]
        index = piece.share + share_index(piece, offsets, None)
        window = fresh.at[piece.next if offsets[0] else piece.g, pl.ds(aligned(origin), piece.unit[3])]
        remote(window, window, share_sems.at[0, index], share_sems.at[1, index], peer("y", 1), j).wait_recv()

    def share_forward(piece, level):
        for offsets in held(piece, level):
            share_wait(piece, offsets)
            share_all(piece, offsets, level)

    def update(k):
        piece = pieces[k]
        total = sum_last(piece)
        normed = rms_scaled(total, atom_gain_ref[...]).astype(BF16)
        hidden = jax.nn.silu(jnp.dot(normed, up_ref[...], preferred_element_type=F32)).astype(BF16)
        new = jnp.dot(hidden, down_ref[...], preferred_element_type=F32).astype(BF16)
        fresh[piece.g, pl.ds(aligned(piece.origin[3]), piece.unit[3])] = new
        share_all(piece, (0, 0, 0), 3)

    near_slots = lax.broadcasted_iota(jnp.int32, (1, half_atoms), 1)

    def merge(g):
        for k in range(chunks):

            @pl.when(away[g])
            def _():
                remote(
                    start.at[g, chunk_rows(k)],
                    recv.at[g, chunk_rows(k)],
                    send_sems.at[g, k],
                    recv_sems.at[g, k],
                    peer("y", 1),
                    j,
                ).wait_recv()

        for first in range(0, chunks, batch):
            column = tile_column(rev_cols, g, first, batch)
            stream[g, chunk_rows(first, batch)] += jnp.dot(
                chosen(column, row_slots), recv[g], preferred_element_type=F32
            )

    def near(g):
        for first in range(0, chunks, batch):
            column = tile_column(tgt_cols, g, first, batch)
            stream[g, chunk_rows(first, batch)] += jnp.dot(
                chosen(column, near_slots + side * half_atoms), fresh[g, half_rows(side)], preferred_element_type=F32
            )

    def finish(g):
        for first in range(0, chunks, batch):
            column = tile_column(tgt_cols, g, first, batch)
            returned = jnp.dot(
                chosen(column, near_slots + (1 - side) * half_atoms),
                fresh[g, half_rows(1 - side)],
                preferred_element_type=F32,
            )
            value = (stream[g, chunk_rows(first, batch)] + returned).astype(BF16)
            out_ref[first : first + batch, g] = value.reshape(batch, rows_sub, width)

    side = digit["y"]
    pace = list(plan["pace"])

    def breathe():
        pump(pace.pop(0) if pace else 1)

    breathe()
    row_scatter()
    breathe()
    for k in range(groups):
        g = lax.rem(i + k + 1, groups)
        for n, first in enumerate(range(0, rows, wide)):
            stream_tile(g, first)
            if k == 0 and n == 0:
                row_across()
            breathe()
        scatter(g)
        if k == groups - 1:
            row_gather()
            row_add()
        sum_send(pieces[k], 0)
        breathe()
    first, last = pieces[0], pieces[-1]
    many = groups > 1
    sum_send(first, 1)
    breathe()
    sum_send(first, 2)
    breathe()
    update(0)
    breathe()
    for k in range(1, groups):
        sum_send(pieces[k], 1)
        breathe()
        share_forward(pieces[k - 1], 2)
        sum_send(pieces[k], 2)
        breathe()
        share_forward(pieces[k - 1], 1)
        update(k)
        breathe()
    share_forward(last, 2)
    breathe()
    share_forward(last, 1)
    pump(len(steps) + 1)
    for g in range(groups):
        merge(g)
    for g in range(groups):
        near(g)
    for k in range(groups):
        share_forward(pieces[k], 0)
    for g in range(groups):
        finish(g)


    @pl.when(jnp.logical_or(off_path, is_helper))
    def _():
        helper_copy().wait_send()

    for g in range(groups):
        for k in range(chunks):
            if k < relayed:

                @pl.when(off_path)
                def _():
                    permute_copy(g, k, False).wait_send()

                for slot in range(half - 1):

                    @pl.when(on_path)
                    def _():
                        forward_copy(slot, g, k).wait_send()

                @pl.when(jnp.logical_and(on_path, away[g]))
                def _():
                    permute_copy(g, k, True).wait_send()
            else:

                @pl.when(away[g])
                def _():
                    permute_copy(g, k, True).wait_send()

    for piece in pieces:
        for level in range(3):
            for step in sum_steps(piece, level):
                sum_copy(piece, level, *step).wait_send()
        for offsets in [(0, 0, 0)] + held(piece, 2) + held(piece, 1):
            below = 3 if offsets == (0, 0, 0) else 2 if offsets in held(piece, 2) else 1
            for level in range(below):
                for offset in range(1, piece.n[level]):
                    share_copy(piece, offsets, level, offset).wait_send()


def shards(
    edge_state,
    atom_state,
    edge_src,
    edge_tgt,
    reverse,
    w_in,
    w_out,
    edge_gain,
    atom_gain,
    atom_up,
    atom_down,
):
    n_src = lax.axis_size("src")
    n_tgt = lax.axis_size("tgt")
    groups = n_src // n_tgt
    edge_rows, width = edge_state.shape
    atoms = atom_state.shape[0]
    rows_sub = edge_rows // (groups * n_src)
    rows = n_src * rows_sub
    parts = [(g, 0, atoms, "ypc") for g in range(groups)]
    plan = {
        "n_src": n_src,
        "n_tgt": n_tgt,
        "groups": groups,
        "parts": parts,
        "batch": 2,
        "wide": min(rows, 512),
        "tall": min(atoms, 256),
        "pace": [2, 1, 1, 0, 0, 0, 0, 0, 0, 1, 0, 0, 1, 1, 1, 1],
    }
    radix = {"y": 2, "p": 2, "c": n_src // 4}
    boxes, packs, sums = 0, 0, 0
    for g, base, size, order in parts:
        n = [radix[dim] for dim in order]
        unit = size
        for level in range(3):
            unit //= n[level]
            boxes += (n[level] - 1) * unit
            packs += (n[level] - 1) * unit if level else 0
            sums += (n[level] - 1) * (n[level + 1] if level < 2 else 1)
    half = n_tgt // 2
    dma = pltpu.SemaphoreType.DMA
    whole = pl.BlockSpec(memory_space=pltpu.VMEM)

    def lines(index):
        return index.reshape(n_src * groups, rows_sub)

    framed = edge_state.reshape(n_src, groups, rows_sub, width)
    out = pl.pallas_call(
        functools.partial(whole_kernel, plan),
        name="block",
        in_specs=[whole] * 11,
        out_specs=whole,
        out_shape=jax.ShapeDtypeStruct(framed.shape, BF16),
        scratch_shapes=[
            pltpu.VMEM((groups, rows, width), BF16),
            pltpu.VMEM((groups, rows, width), F32),
            pltpu.VMEM((groups, rows, width), BF16),
            pltpu.VMEM((half - 1, groups, rows // 2, width), BF16),
            pltpu.VMEM((groups, rows, width), BF16),
            pltpu.VMEM((groups, atoms, width), BF16),
            pltpu.VMEM((boxes, width), BF16),
            pltpu.VMEM((packs, width), BF16),
            pltpu.VMEM((groups, atoms, width), BF16),
            pltpu.VMEM((atoms, width), BF16),
            pltpu.VMEM((atoms // 2, width), BF16),
            pltpu.VMEM((half + 1, atoms // 2, width), BF16),
            dma((groups, n_src)),
            dma((groups, n_src)),
            dma((half - 1, groups, n_src // 2)),
            dma((half - 1, groups, n_src // 2)),
            dma((2, sums)),
            dma((2, len(parts) * n_src)),
            dma((2, half + 1)),
        ],
        compiler_params=pltpu.CompilerParams(
            collective_id=0, has_side_effects=True, vmem_limit_bytes=56 * 2**20
        ),
    )(
        framed,
        atom_state,
        lines(edge_src),
        lines(edge_tgt),
        lines(reverse),
        w_in,
        w_out,
        edge_gain,
        atom_gain.reshape(1, width),
        atom_up,
        atom_down,
    )
    return out.reshape(edge_rows, width)


def solution(mesh):
    in_specs = (
        P(("src", "tgt"), None),
        P("src", None),
        P(("src", "tgt")),
        P(("src", "tgt")),
        P(("src", "tgt")),
        P(),
        P(),
        P(),
        P(),
        P(),
        P(),
    )
    out_specs = P(("src", "tgt"), None)
    return jax.shard_map(shards, mesh=mesh, in_specs=in_specs, out_specs=out_specs, check_vma=False)
```

```python
import functools

import jax
import jax.numpy as jnp
from jax import lax
from jax.experimental import pallas as pl
from jax.experimental.pallas import tpu as pltpu
from jax.sharding import PartitionSpec as P

F32 = jnp.float32
BF16 = jnp.bfloat16
MESH = pl.DeviceIdType.MESH


def rms_scaled(values, scales):
    return values * lax.rsqrt(jnp.mean(values * values, axis=-1, keepdims=True) + 1e-06) * scales


def whole_kernel(
    plan,
    edge_ref,
    atom_ref,
    src_ref,
    tgt_ref,
    rev_ref,
    w_in_ref,
    w_out_ref,
    gain_ref,
    atom_gain_ref,
    up_ref,
    down_ref,
    out_ref,
    start,
    stream,
    recv,
    relay,
    message,
    part,
    box,
    pack,
    fresh,
    row_part,
    row_pack,
    row_box,
    send_sems,
    recv_sems,
    relay_sems,
    forward_sems,
    sum_sems,
    share_sems,
    row_sems,
):
    n_src, n_tgt, groups = plan["n_src"], plan["n_tgt"], plan["groups"]
    slices, _, rows_sub, width = edge_ref.shape
    rows = slices * rows_sub
    atoms = atom_ref.shape[0]
    layers = w_in_ref.shape[0]
    half = n_tgt // 2
    chunks = slices
    relayed = chunks // 2
    i = lax.axis_index("src")
    j = lax.axis_index("tgt")
    home = i // groups
    phase = lax.rem(i, groups)
    on_path = j // 2 == home // 2
    off_path = jnp.logical_not(on_path)
    away = [i != j * groups + g for g in range(groups)]

    def remote(source, target, send_sem, recv_sem, row, col):
        return pltpu.make_async_remote_copy(
            src_ref=source,
            dst_ref=target,
            send_sem=send_sem,
            recv_sem=recv_sem,
            device_id={"src": row, "tgt": col},
            device_id_type=MESH,
        )

    radix = {"y": 2, "p": 2, "c": n_src // 4}
    scale = {"y": 1, "p": 2, "c": 4}
    digit = {"y": lax.rem(i, 2), "p": lax.rem(i // 2, 2), "c": i // 4}

    def peer(dim, offset):
        turned = lax.rem(digit[dim] + offset, radix[dim])
        return i + (turned - digit[dim]) * scale[dim]

    barrier = pltpu.get_barrier_semaphore()

    def greet(row, col):
        pl.semaphore_signal(barrier, inc=1, device_id={"src": row, "tgt": col}, device_id_type=MESH)

    greet(i, j + 1 - 2 * lax.rem(j, 2))
    count = jnp.int32(1)
    for dim in "ypc":
        for offset in range(1, radix[dim]):
            greet(peer(dim, offset), j)
            count += 1
    for g in range(groups):

        @pl.when(away[g])
        def _():
            greet(j * groups + g, home)

        count += away[g].astype(jnp.int32)

        @pl.when(off_path)
        def _():
            greet(j * groups + g, j // 2 * 2 + lax.rem(home, 2))

    for slot in range(half - 1):
        source_col = lax.rem(j // 2 + slot + 1, half) * 2 + lax.rem(j, 2)

        @pl.when(on_path)
        def _():
            greet(i, source_col)

    count += jnp.where(on_path, (half - 1) * groups, 1)
    src_cols = src_ref[...].T
    reverse = rev_ref[...]
    rev_cols = (lax.div(reverse, groups * rows_sub) * rows_sub + lax.rem(reverse, rows_sub)).T
    tgt_cols = tgt_ref[...].T

    def tile_column(cols, g, first, number):
        return jnp.concatenate(
            [cols[:, n * groups + g : n * groups + g + 1] for n in range(first, first + number)], axis=0
        )

    def chosen(column, slots):
        return jnp.where(column == slots, 1.0, 0.0).astype(BF16)

    atom_slots = lax.broadcasted_iota(jnp.int32, (1, atoms), 1)
    row_slots = lax.broadcasted_iota(jnp.int32, (1, rows), 1)

    def chunk_rows(k, number=1):
        return pl.ds(k * rows_sub, number * rows_sub)

    def permute_copy(g, k, direct):
        source = start.at[g, chunk_rows(k)]
        if direct:
            return remote(
                source, recv.at[phase, chunk_rows(k)], send_sems.at[g, k], recv_sems.at[phase, k], j * groups + g, home
            )
        slot = lax.rem(j // 2 - home // 2 + half, half) - 1
        slot = jnp.maximum(slot, 0)
        return remote(
            source,
            relay.at[slot, g, chunk_rows(k)],
            send_sems.at[g, k],
            relay_sems.at[slot, g, k],
            i,
            home // 2 * 2 + lax.rem(j, 2),
        )

    def permute_send(g, k):
        if k < relayed:

            @pl.when(off_path)
            def _():
                permute_copy(g, k, False).start()

            @pl.when(jnp.logical_and(on_path, away[g]))
            def _():
                permute_copy(g, k, True).start()
        else:

            @pl.when(away[g])
            def _():
                permute_copy(g, k, True).start()

    def forward_copy(slot, g, k):
        column = lax.rem(j // 2 + slot + 1, half) * 2 + lax.rem(j, 2)
        return remote(
            relay.at[slot, g, chunk_rows(k)],
            recv.at[phase, chunk_rows(k)],
            forward_sems.at[slot, g, k],
            recv_sems.at[phase, k],
            column * groups + g,
            home,
        )

    def arrival(slot, g, k):
        return remote(
            relay.at[slot, g, chunk_rows(k)],
            relay.at[slot, g, chunk_rows(k)],
            forward_sems.at[slot, g, k],
            relay_sems.at[slot, g, k],
            i,
            lax.rem(j + 2, n_tgt),
        )

    def forward(g, k):
        for slot in range(half - 1):

            @pl.when(on_path)
            def _():
                arrival(slot, g, k).wait_recv()
                forward_copy(slot, g, k).start()

    batch = plan["batch"]
    for first in range(0, chunks, batch):
        for g in range(groups):
            column = tile_column(src_cols, g, first, batch)
            sources = jnp.dot(chosen(column, atom_slots), atom_ref[...], preferred_element_type=F32)
            edges = edge_ref[first : first + batch, g].reshape(batch * rows_sub, width).astype(F32)
            value = (edges + sources).astype(BF16)
            start[g, chunk_rows(first, batch)] = value

            @pl.when(jnp.logical_not(away[g]))
            def _():
                recv[g, chunk_rows(first, batch)] = value

    pl.semaphore_wait(barrier, count)

    steps = [(g, k) for k in range(relayed) for g in range(groups)]
    behind = []

    def pump(number):
        for _ in range(number):
            if behind:
                forward(*behind.pop(0))
            if steps:
                g, k = steps.pop(0)
                permute_send(g, k)
                permute_send(g, relayed + k)
                behind.append((g, k))

    tall = plan["tall"]
    core = lax.rem(j, 2)
    half_atoms = atoms // 2
    is_root = home == j
    is_helper = jnp.logical_and(on_path, jnp.logical_not(is_root))

    def aligned(value):
        return pl.multiple_of(value, 16)

    def index_line(ref, g):
        return jnp.concatenate([ref[pl.ds(n * groups + g, 1), :] for n in range(slices)], axis=1)

    def picks(line, first):
        slots = lax.broadcasted_iota(jnp.int32, (tall, line.shape[1]), 0) + first
        return jnp.where(slots == line, 1.0, 0.0).astype(BF16)

    def half_rows(which):
        return pl.ds(aligned(which * half_atoms), half_atoms)

    def core_copy():
        return remote(
            row_part.at[half_rows(1 - core)], row_box.at[0], row_sems.at[0, 0], row_sems.at[1, 0], i, j + 1 - 2 * core
        )

    def across_copy():
        slot = jnp.maximum(lax.rem(j // 2 - home // 2 + half, half) - 1, 0)
        return remote(
            row_pack, row_box.at[2 + slot], row_sems.at[0, 1], row_sems.at[1, 2 + slot], i, home // 2 * 2 + core
        )

    def helper_copy():
        return remote(row_pack, row_box.at[1], row_sems.at[0, 1], row_sems.at[1, 1], i, home)

    def row_scatter():
        lines = [index_line(src_ref, g) for g in range(groups)]
        for first in range(0, atoms, tall):
            total = jnp.dot(picks(lines[0], first), start[0], preferred_element_type=F32)
            for g in range(1, groups):
                total = total + jnp.dot(picks(lines[g], first), start[g], preferred_element_type=F32)
            row_part[pl.ds(first, tall)] = total.astype(BF16)
        core_copy().start()

    def row_across():
        core_copy().wait()

        @pl.when(off_path)
        def _():
            row_pack[...] = (row_part[half_rows(core)].astype(F32) + row_box[0].astype(F32)).astype(BF16)
            across_copy().start()

    def row_total():
        total = row_part[half_rows(core)].astype(F32) + row_box[0].astype(F32)
        for slot in range(half - 1):
            total = total + row_box[2 + slot].astype(F32)
        return total

    def row_gather():
        for slot in range(half - 1):

            @pl.when(on_path)
            def _():
                remote(
                    row_pack, row_box.at[2 + slot], row_sems.at[0, 1], row_sems.at[1, 2 + slot], i, j + 1 - 2 * core
                ).wait_recv()

        @pl.when(is_helper)
        def _():
            row_pack[...] = row_total().astype(BF16)
            helper_copy().start()

    def row_add():
        @pl.when(is_root)
        def _():
            mine, other = half_rows(core), half_rows(1 - core)
            part[phase, mine] = (part[phase, mine].astype(F32) + row_total()).astype(BF16)
            remote(
                row_pack, row_box.at[1], row_sems.at[0, 1], row_sems.at[1, 1], i, j + 1 - 2 * core
            ).wait_recv()
            part[phase, other] = (part[phase, other].astype(F32) + row_box[1].astype(F32)).astype(BF16)

    wide = plan["wide"]

    def stream_tile(g, first):
        values = start[g, pl.ds(first, wide)].astype(F32)
        for layer in range(layers):
            normed = rms_scaled(values, gain_ref[layer : layer + 1]).astype(BF16)
            hidden = jax.nn.silu(jnp.dot(normed, w_in_ref[layer], preferred_element_type=F32)).astype(BF16)
            values = values + jnp.dot(hidden, w_out_ref[layer], preferred_element_type=F32)
        stream[g, pl.ds(first, wide)] = values
        message[g, pl.ds(first, wide)] = values.astype(BF16)

    def scatter(g):
        line = index_line(tgt_ref, g)
        for first in range(0, atoms, tall):
            part[g, pl.ds(first, tall)] = jnp.dot(
                picks(line, first), message[g], preferred_element_type=F32
            ).astype(BF16)

    class Piece:
        pass

    pieces = []
    sums, shares, boxes, packs = 0, 0, 0, 0
    for k, base, size, order in plan["parts"]:
        piece = Piece()
        piece.k, piece.base, piece.size, piece.order = k, base, size, order
        piece.g, piece.next = lax.rem(i + k, groups), lax.rem(i + k + 1, groups)
        piece.n = [radix[dim] for dim in order]
        piece.d = [digit[dim] for dim in order]
        piece.unit = [size]
        for n in piece.n:
            piece.unit.append(piece.unit[-1] // n)
        piece.origin = [jnp.int32(base)]
        for level in range(3):
            piece.origin.append(piece.origin[-1] + piece.d[level] * piece.unit[level + 1])
        piece.box, piece.pack, piece.sum = [], [], []
        for level in range(3):
            piece.box.append(boxes)
            piece.pack.append(packs)
            piece.sum.append(sums)
            boxes += (piece.n[level] - 1) * piece.unit[level + 1]
            packs += (piece.n[level] - 1) * piece.unit[level + 1] if level else 0
            sums += (piece.n[level] - 1) * (piece.n[level + 1] if level < 2 else 1)
        piece.route = (2, 1, 0)
        piece.share = shares
        shares += n_src
        pieces.append(piece)

    def value_at(piece, level, origin, size):
        total = part[piece.g, pl.ds(aligned(origin), size)].astype(F32)
        for lower in range(level):
            for offset in range(1, piece.n[lower]):
                place = piece.box[lower] + (offset - 1) * piece.unit[lower + 1] + origin - piece.origin[lower + 1]
                total = total + box[pl.ds(aligned(place), size)].astype(F32)
        return total

    def sum_steps(piece, level):
        unit = piece.unit[level + 1]
        fan = piece.n[level + 1] if level < 2 else 1
        inner = unit // fan
        for turn in range(fan):
            for offset in range(1, piece.n[level]):
                theirs = lax.rem(piece.d[level] + offset, piece.n[level])
                if level < 2:
                    spot = lax.rem(piece.d[level + 1] + turn + 1, fan) * inner
                else:
                    spot = jnp.int32(0)
                yield turn, offset, piece.origin[level] + theirs * unit + spot, spot, inner

    def sum_copy(piece, level, turn, offset, origin, spot, inner):
        fan = piece.n[level + 1] if level < 2 else 1
        if level == 0:
            source = part.at[piece.next, pl.ds(aligned(origin), inner)]
        else:
            place = piece.pack[level] + (offset - 1) * piece.unit[level + 1] + spot
            source = pack.at[pl.ds(aligned(place), inner)]
        target = box.at[pl.ds(aligned(piece.box[level] + (offset - 1) * piece.unit[level + 1] + spot), inner)]
        index = piece.sum[level] + (offset - 1) * fan + turn
        return remote(source, target, sum_sems.at[0, index], sum_sems.at[1, index], peer(piece.order[level], offset), j)

    def sum_wait(piece, level, turn):
        for step in sum_steps(piece, level):
            if step[0] == turn:
                sum_copy(piece, level, *step).wait_recv()

    def sum_send(piece, level):
        ready = set()
        fan = piece.n[level]
        for step in sum_steps(piece, level):
            turn, offset, origin, spot, inner = step
            if level:
                need = (offset - 1) % fan
                if need not in ready:
                    ready.add(need)
                    sum_wait(piece, level - 1, need)
                    if level > 1:
                        pass
                place = piece.pack[level] + (offset - 1) * piece.unit[level + 1] + spot
                pack[pl.ds(aligned(place), inner)] = value_at(piece, level, origin, inner).astype(BF16)
            sum_copy(piece, level, *step).start()
        if level:
            for turn in range(fan):
                if turn not in ready:
                    ready.add(turn)
                    piece_last = turn
                    sum_wait(piece, level - 1, piece_last)

    def sum_last(piece):
        sum_wait(piece, 2, 0)
        return value_at(piece, 3, piece.origin[3], piece.unit[3])

    def share_index(piece, offsets, dim_level):
        n = piece.n
        return ((offsets[0] * n[1]) + offsets[1]) * n[2] + offsets[2]

    def share_copy(piece, offsets, level, offset):
        origin = jnp.int32(piece.base)
        for low in range(3):
            owner = lax.rem(piece.d[low] - offsets[low] + piece.n[low], piece.n[low])
            origin = origin + owner * piece.unit[low + 1]
        there = list(offsets)
        there[level] = offset
        index = piece.share + share_index(piece, there, level)
        window = fresh.at[piece.next if offsets[0] else piece.g, pl.ds(aligned(origin), piece.unit[3])]
        return remote(window, window, share_sems.at[0, index], share_sems.at[1, index], peer(piece.order[level], offset), j)

    def held(piece, level):
        place = piece.route.index(level)
        options = [(0,), (0,), (0,)]
        options[level] = tuple(range(1, piece.n[level]))
        for ahead in piece.route[:place]:
            options[ahead] = tuple(range(piece.n[ahead]))
        return [(a, b, c) for a in options[0] for b in options[1] for c in options[2]]

    def onward(piece, offsets):
        taken = [place for place, level in enumerate(piece.route) if offsets[level]]
        return piece.route[taken[-1] + 1 if taken else 0 :]

    def share_all(piece, offsets):
        for level in onward(piece, offsets):
            for offset in range(1, piece.n[level]):
                share_copy(piece, offsets, level, offset).start()

    def share_wait(piece, offsets):
        origin = jnp.int32(piece.base)
        for low in range(3):
            owner = lax.rem(piece.d[low] - offsets[low] + piece.n[low], piece.n[low])
            origin = origin + owner * piece.unit[low + 1]
        index = piece.share + share_index(piece, offsets, None)
        window = fresh.at[piece.next if offsets[0] else piece.g, pl.ds(aligned(origin), piece.unit[3])]
        remote(window, window, share_sems.at[0, index], share_sems.at[1, index], peer("y", 1), j).wait_recv()

    def share_forward(piece, level):
        for offsets in held(piece, level):
            share_wait(piece, offsets)
            share_all(piece, offsets)

    def update(k):
        piece = pieces[k]
        total = sum_last(piece)
        normed = rms_scaled(total, atom_gain_ref[...]).astype(BF16)
        hidden = jax.nn.silu(jnp.dot(normed, up_ref[...], preferred_element_type=F32)).astype(BF16)
        new = jnp.dot(hidden, down_ref[...], preferred_element_type=F32).astype(BF16)
        fresh[piece.g, pl.ds(aligned(piece.origin[3]), piece.unit[3])] = new
        share_all(piece, (0, 0, 0))

    near_slots = lax.broadcasted_iota(jnp.int32, (1, half_atoms), 1)

    def merge(g):
        for k in range(chunks):

            @pl.when(away[g])
            def _():
                remote(
                    start.at[g, chunk_rows(k)],
                    recv.at[g, chunk_rows(k)],
                    send_sems.at[g, k],
                    recv_sems.at[g, k],
                    peer("y", 1),
                    j,
                ).wait_recv()

        for first in range(0, chunks, batch):
            column = tile_column(rev_cols, g, first, batch)
            stream[g, chunk_rows(first, batch)] += jnp.dot(
                chosen(column, row_slots), recv[g], preferred_element_type=F32
            )

    def target_column(g, first):
        column = tile_column(tgt_cols, 0, first, batch)
        for group in range(1, groups):
            column = jnp.where(g == group, tile_column(tgt_cols, group, first, batch), column)
        return column

    def returned(g, which, first):
        return jnp.dot(
            chosen(target_column(g, first), near_slots + which * half_atoms),
            fresh[g, half_rows(which)],
            preferred_element_type=F32,
        )

    def near(g, which):
        for first in range(0, chunks, batch):
            stream[g, chunk_rows(first, batch)] += returned(g, which, first)

    def finish(g, which):
        for first in range(0, chunks, batch):
            value = (stream[g, chunk_rows(first, batch)] + returned(g, which, first)).astype(BF16)
            out_ref[first : first + batch, g] = value.reshape(batch, rows_sub, width)

    side = digit["y"]
    pace = list(plan["pace"])

    def breathe():
        pump(pace.pop(0) if pace else 1)

    breathe()
    row_scatter()
    breathe()
    for k in range(groups):
        g = lax.rem(i + k + 1, groups)
        for n, first in enumerate(range(0, rows, wide)):
            stream_tile(g, first)
            if k == 0 and n == 0:
                row_across()
            breathe()
        scatter(g)
        if k == groups - 1:
            row_gather()
            row_add()
        sum_send(pieces[k], 0)
        breathe()
    first, last = pieces[0], pieces[-1]
    many = groups > 1
    sum_send(first, 1)
    breathe()
    sum_send(first, 2)
    breathe()
    update(0)
    breathe()
    for k in range(1, groups):
        sum_send(pieces[k], 1)
        breathe()
        share_forward(pieces[k - 1], 2)
        sum_send(pieces[k], 2)
        breathe()
        share_forward(pieces[k - 1], 1)
        update(k)
        breathe()
    share_forward(last, last.route[0])
    breathe()
    share_forward(last, last.route[1])
    pump(len(steps) + 1)
    for g in range(groups):
        merge(g)
    near(first.g, side)
    share_forward(first, 0)
    if many:
        near(last.g, side)
        finish(first.next, 1 - side)
        share_forward(last, 0)
        finish(last.next, 1 - side)
    else:
        finish(first.next, 1 - side)


    @pl.when(jnp.logical_or(off_path, is_helper))
    def _():
        helper_copy().wait_send()

    for g in range(groups):
        for k in range(chunks):
            if k < relayed:

                @pl.when(off_path)
                def _():
                    permute_copy(g, k, False).wait_send()

                for slot in range(half - 1):

                    @pl.when(on_path)
                    def _():
                        forward_copy(slot, g, k).wait_send()

                @pl.when(jnp.logical_and(on_path, away[g]))
                def _():
                    permute_copy(g, k, True).wait_send()
            else:

                @pl.when(away[g])
                def _():
                    permute_copy(g, k, True).wait_send()

    for piece in pieces:
        for level in range(3):
            for step in sum_steps(piece, level):
                sum_copy(piece, level, *step).wait_send()
        for offsets in [(0, 0, 0)] + held(piece, 0) + held(piece, 1) + held(piece, 2):
            for level in onward(piece, offsets):
                for offset in range(1, piece.n[level]):
                    share_copy(piece, offsets, level, offset).wait_send()


def shards(
    edge_state,
    atom_state,
    edge_src,
    edge_tgt,
    reverse,
    w_in,
    w_out,
    edge_gain,
    atom_gain,
    atom_up,
    atom_down,
):
    n_src = lax.axis_size("src")
    n_tgt = lax.axis_size("tgt")
    groups = n_src // n_tgt
    edge_rows, width = edge_state.shape
    atoms = atom_state.shape[0]
    rows_sub = edge_rows // (groups * n_src)
    rows = n_src * rows_sub
    parts = [(g, 0, atoms, "ypc") for g in range(groups)]
    plan = {
        "n_src": n_src,
        "n_tgt": n_tgt,
        "groups": groups,
        "parts": parts,
        "batch": 4,
        "wide": min(rows, 512),
        "tall": min(atoms, 512),
        "pace": [2, 1, 1, 0, 0, 0, 0, 0, 0, 1, 0, 0, 1, 1, 1, 1],
    }
    radix = {"y": 2, "p": 2, "c": n_src // 4}
    boxes, packs, sums = 0, 0, 0
    for g, base, size, order in parts:
        n = [radix[dim] for dim in order]
        unit = size
        for level in range(3):
            unit //= n[level]
            boxes += (n[level] - 1) * unit
            packs += (n[level] - 1) * unit if level else 0
            sums += (n[level] - 1) * (n[level + 1] if level < 2 else 1)
    half = n_tgt // 2
    dma = pltpu.SemaphoreType.DMA
    whole = pl.BlockSpec(memory_space=pltpu.VMEM)

    def lines(index):
        return index.reshape(n_src * groups, rows_sub)

    framed = edge_state.reshape(n_src, groups, rows_sub, width)
    out = pl.pallas_call(
        functools.partial(whole_kernel, plan),
        name="block",
        in_specs=[whole] * 11,
        out_specs=whole,
        out_shape=jax.ShapeDtypeStruct(framed.shape, BF16),
        scratch_shapes=[
            pltpu.VMEM((groups, rows, width), BF16),
            pltpu.VMEM((groups, rows, width), F32),
            pltpu.VMEM((groups, rows, width), BF16),
            pltpu.VMEM((half - 1, groups, rows // 2, width), BF16),
            pltpu.VMEM((groups, rows, width), BF16),
            pltpu.VMEM((groups, atoms, width), BF16),
            pltpu.VMEM((boxes, width), BF16),
            pltpu.VMEM((packs, width), BF16),
            pltpu.VMEM((groups, atoms, width), BF16),
            pltpu.VMEM((atoms, width), BF16),
            pltpu.VMEM((atoms // 2, width), BF16),
            pltpu.VMEM((half + 1, atoms // 2, width), BF16),
            dma((groups, n_src)),
            dma((groups, n_src)),
            dma((half - 1, groups, n_src // 2)),
            dma((half - 1, groups, n_src // 2)),
            dma((2, sums)),
            dma((2, len(parts) * n_src)),
            dma((2, half + 1)),
        ],
        compiler_params=pltpu.CompilerParams(
            collective_id=0, has_side_effects=True, vmem_limit_bytes=56 * 2**20
        ),
    )(
        framed,
        atom_state,
        lines(edge_src),
        lines(edge_tgt),
        lines(reverse),
        w_in,
        w_out,
        edge_gain,
        atom_gain.reshape(1, width),
        atom_up,
        atom_down,
    )
    return out.reshape(edge_rows, width)


def solution(mesh):
    in_specs = (
        P(("src", "tgt"), None),
        P("src", None),
        P(("src", "tgt")),
        P(("src", "tgt")),
        P(("src", "tgt")),
        P(),
        P(),
        P(),
        P(),
        P(),
        P(),
    )
    out_specs = P(("src", "tgt"), None)
    return jax.shard_map(shards, mesh=mesh, in_specs=in_specs, out_specs=out_specs, check_vma=False)
```
